32 devices in a mesh: shot: 2 (over x), freq: 8 (over z, y), tile: 2 (over core).
Axes of the slice: x: 2, y: 2, z: 4, core: 2. Of those that a mesh axis runs over, the one named last changes fastest.
Arguments:
- source_field: float32 [4, 8, 64, 1024], P('shot', 'freq', 'tile'), parts along dimension 0, may hold values from -6 to 6
- receiver_field: float32 [4, 8, 64, 1024], P('shot', 'freq', 'tile'), parts along dimension 0, may hold values from -6 to 6
- slowness: float32 [3, 64, 1024], P(None, 'tile', 'freq'), may hold values from 0.5 to 2
- omegas: float32 [8], P('freq'), may hold values from 1.5 to 5
Outputs:
- image_steps: float32 [6, 64, 1024], P('shot', 'tile'), parts along dimension 0
- illumination: float32 [6, 64, 1024], P('shot', 'tile'), parts along dimension 0
The draws below stay inside these ranges and needn't reach their ends.
There are 2 independent parts, one for each index of `shot`. The reference program is written for one: setup_inputs(seed, part) draws one part's arguments, and reference() takes and returns one part's arrays. A program takes and returns all parts, laid end to end along the dimension named above; an argument that names none is the same for every part. Nothing has to cross between parts.
All inputs are finite; a program needn't handle non-finite values.
Results may differ from the reference program's by a relative error of at most 0.0003.
Values sent between devices are 32-bit elements; how exact they have to be, the bound alone decides.
A program may use at most 64 MiB of HBM per device.

```python
import math
import jax
import jax.numpy as jnp
from jax import lax

NY = 1024
STEPS = 3
TERMS = 10
NODES = 16
NF = 8
NX = 64


def block_levels(rng, dims, shards, least, high):
    gain = 1.0
    for axis_at, shards_of in shards:
        steps = jax.random.uniform(jax.random.fold_in(jax.random.fold_in(rng, 6), axis_at), (shards_of,), jnp.float32, least / len(shards), high / len(shards))
        gain = gain * jnp.repeat(jnp.exp(steps), dims[axis_at] // shards_of).reshape((-1,) + (1,) * (len(dims) - 1 - axis_at))
    return gain


def centred(key, extent, width, most, split=(), held_as=jnp.bfloat16):
    level = block_levels(key, extent, split, -0.22, 0.18) if split else 1.0
    array = jax.random.normal(key, extent, jnp.float32) * width * level
    return jnp.minimum(jnp.maximum(array, -most), most).astype(held_as)


def setup_inputs(seed: int = 0, part: int = 0) -> dict:
    keys = jax.random.split(jax.random.key(seed), 5)
    own_keys = jax.random.split(jax.random.fold_in(keys[4], part), 5)
    return {
        "source_field": centred(own_keys[0], (2, NF, NX, NY), 1.0, 6.0, ((1, 8), (2, 2)), jnp.float32),
        "receiver_field": centred(own_keys[1], (2, NF, NX, NY), 1.0, 6.0, ((1, 8), (2, 2)), jnp.float32),
        "slowness": jnp.clip(0.5 + 1.5 * jax.random.uniform(keys[2], (STEPS, NX, NY), jnp.float32) ** block_levels(keys[2], (STEPS, NX, NY), ((1, 2), (2, 8)), -0.2, 0.2), 0.5, 2.0),
        "omegas": jnp.clip(jnp.exp(math.log(5.0) - 1.2039728 * jax.random.uniform(keys[3], (NF,), jnp.float32) ** block_levels(keys[3], (NF,), ((0, 8),), -0.2, 0.2)), 1.5, 5.0),
    }


def mcclellan_rows(padded):
    along_x = 0.5 * padded[:, :, :-2] + padded[:, :, 1:-1] + 0.5 * padded[:, :, 2:]
    widened = jnp.pad(along_x, ((0, 0), (0, 0), (0, 0), (1, 1)))
    along_y = 0.5 * widened[..., :-2] + widened[..., 1:-1] + 0.5 * widened[..., 2:]
    return 0.5 * along_y - padded[:, :, 1:-1]

def mcclellan_full(fields):
    return mcclellan_rows(jnp.pad(fields, ((0, 0), (0, 0), (1, 1), (0, 0))))

def coefficients(omega_values, slow_slab):
    node_angles = (jnp.arange(NODES, dtype=jnp.float32) + 0.5) * (math.pi / NODES)
    orders = jnp.arange(TERMS, dtype=jnp.float32)
    weights = jnp.where(orders == 0, 1.0, 2.0) / NODES
    cheb_table = jnp.cos(node_angles[:, None] * orders[None, :]) * weights[None, :]
    phase_arg = omega_values[:, None, None, None] * jnp.cos(node_angles)[None, :, None, None] * slow_slab[None, None]
    coef_real = jnp.einsum('fmxy,mn->fnxy', jnp.cos(phase_arg), cheb_table, precision=lax.Precision.HIGHEST)
    coef_imag = jnp.einsum('fmxy,mn->fnxy', jnp.sin(phase_arg), cheb_table, precision=lax.Precision.HIGHEST)
    return (coef_real, coef_imag)

def apply_terms(summed, coef_real, coef_imag, cheb_term):
    source_real, source_imag, receiver_real, receiver_imag = (cheb_term[0], cheb_term[1], cheb_term[2], cheb_term[3])
    return summed + jnp.stack([coef_real * source_real - coef_imag * source_imag, coef_real * source_imag + coef_imag * source_real, coef_real * receiver_real + coef_imag * receiver_imag, coef_real * receiver_imag - coef_imag * receiver_real])

def extrapolate(fields, coef_real, coef_imag):
    prev_term = fields
    this_term = mcclellan_full(fields)
    summed = apply_terms(jnp.zeros_like(fields), coef_real[:, 0], coef_imag[:, 0], prev_term)
    summed = apply_terms(summed, coef_real[:, 1], coef_imag[:, 1], this_term)
    for term_order in range(2, TERMS):
        next_term = 2.0 * mcclellan_full(this_term) - prev_term
        summed = apply_terms(summed, coef_real[:, term_order], coef_imag[:, term_order], next_term)
        prev_term, this_term = (this_term, next_term)
    return summed

def reference(source_field, receiver_field, slowness, omegas):
    fields = jnp.concatenate([source_field, receiver_field], 0)
    image_list = []
    energy_list = []
    for depth_index in range(STEPS):
        coef_real, coef_imag = coefficients(omegas, slowness[depth_index])
        fields = extrapolate(fields, coef_real, coef_imag)
        image_list.append(lax.optimization_barrier(jnp.sum(fields[0] * fields[2] + fields[1] * fields[3], axis=0)) / math.sqrt(NF))
        energy_list.append(lax.optimization_barrier(jnp.sum(fields[0] * fields[0] + fields[1] * fields[1], axis=0)) / NF)
    return (jnp.stack(image_list), jnp.stack(energy_list))
```

```python
import functools
import math

import jax
import jax.numpy as jnp
import numpy as np
from jax import lax
from jax.experimental import pallas as pl
from jax.experimental.pallas import tpu as pltpu
from jax.sharding import PartitionSpec as P

TERMS = 10
NODES = 16
HALF = NODES // 2
SUB, LANE = 8, 128
HALO = 16
PAD = 8
MESH = pl.DeviceIdType.MESH
ORDER_US, ACC_US = 0.25, 0.5
LAGS = (3.0, 6.5, 10.0, 13.0)

SIN_POLY = (3.14159258, -5.16770688, 2.55003137, -0.59804516, 0.07722009)
COS_POLY = (0.99999995, -4.93479286, 4.0584119, -1.33188005, 0.21969657)


def horner(coefs, z):
    out = coefs[-1] * z + coefs[-2]
    for c in reversed(coefs[:-2]):
        out = out * z + c
    return out


def folded_coefficients(u):
    theta = [math.pi * (m + 0.5) / NODES for m in range(HALF)]
    cosines, sines = [], []
    for m in range(HALF):
        y = u * (math.cos(theta[m]) / (2 * math.pi))
        g = y - jnp.round(y)
        z = g * g
        s = horner(SIN_POLY, z) * g
        c = horner(COS_POLY, z)
        twice = s + s
        cosines.append(1.0 - twice * s)
        sines.append(twice * c)
    weight = [2.0 * (1.0 if n == 0 else 2.0) / NODES for n in range(TERMS)]
    out = [None] * TERMS
    sums = [cosines[m] + cosines[HALF - 1 - m] for m in range(HALF // 2)]
    diffs = [cosines[m] - cosines[HALF - 1 - m] for m in range(HALF // 2)]
    for n in range(0, TERMS, 2):
        terms = sums if (n // 2) % 2 == 0 else diffs
        total = None
        for m in range(HALF // 2):
            term = terms[m] * (weight[n] * math.cos(n * theta[m]))
            total = term if total is None else total + term
        out[n] = total
    for n in range(1, TERMS, 2):
        total = None
        for m in range(HALF):
            term = sines[m] * (weight[n] * math.cos(n * theta[m]))
            total = term if total is None else total + term
        out[n] = total
    return out


def kernel(cfg, src_ref, rec_ref, slow_ref, omega_ref, image_ref, energy_ref, field, gathered, part,
           recv1, acc1, recv2, result, load_sem, own_sem, out_sem, slow_send, slow_recv,
           halo_send, halo_recv, s1_send, s1_recv, s2_send, s2_recv,
           gz_send, gz_recv, gy_send, gy_recv):
    n, g1, g2, rows, width, steps, freq_total, cols, chunk_cols, unit_rows = cfg
    blocks = width // LANE
    per_row = width // chunk_cols
    units = steps * (rows // unit_rows)
    fi = lax.axis_index("freq")
    ti = lax.axis_index("tile")
    yi, zi = lax.rem(fi, g1), lax.div(fi, g1)
    other_y = g1 - 1 - yi

    def freq_at(y, z):
        return {"freq": z * g1 + y}

    def own(r):
        return pl.multiple_of(PAD + PAD * ti + r, SUB)

    loads = []
    for c in range(blocks):
        lanes = pl.ds(c * LANE, LANE)
        loads.append(pltpu.make_async_copy(
            src_ref.at[:, :, lanes], field.at[0, 0:2, c, pl.ds(own(0), rows)], load_sem.at[0, c]))
        loads.append(pltpu.make_async_copy(
            rec_ref.at[:, :, lanes], field.at[0, 2:4, c, pl.ds(own(0), rows)], load_sem.at[1, c]))
    own_load = pltpu.make_async_copy(slow_ref, gathered.at[fi], own_sem)
    for copy in loads:
        copy.start()
    own_load.start()

    barrier = pltpu.get_barrier_semaphore()
    for j in range(1, n):
        pl.semaphore_signal(barrier, inc=1, device_id={"freq": lax.rem(fi + j, n)}, device_id_type=MESH)
    pl.semaphore_signal(barrier, inc=1, device_id={"tile": 1 - ti}, device_id_type=MESH)

    zero = jnp.zeros((4, blocks, SUB, LANE), jnp.float32)
    low, high = pl.ds(0, SUB), pl.ds(PAD + rows + SUB, SUB)
    edge = pl.ds(pl.multiple_of((PAD + rows + SUB) * ti, SUB), SUB)
    for d in range(steps):
        field[d, :, :, edge, :] = zero
    for t in range(1, TERMS):
        field[steps - 1 + t, :, :, low, :] = zero
        field[steps - 1 + t, :, :, high, :] = zero

    for copy in loads:
        copy.wait()
    pl.semaphore_wait(barrier, n)

    def halo_copy(d):
        src = pl.multiple_of(jnp.where(ti == 0, PAD + rows - HALO, PAD + PAD), SUB)
        dst = pl.multiple_of(jnp.where(ti == 0, PAD + rows, 0), SUB)
        far = pl.multiple_of(jnp.where(ti == 0, 0, PAD + rows), SUB)
        return pltpu.make_async_remote_copy(
            src_ref=field.at[d, :, :, pl.ds(src, HALO)], dst_ref=field.at[d, :, :, pl.ds(far, HALO)],
            send_sem=halo_send.at[d], recv_sem=halo_recv.at[d],
            device_id={"tile": 1 - ti}, device_id_type=MESH)

    def slow_copy(d, slot, j, target):
        return pltpu.make_async_remote_copy(
            src_ref=slow_ref.at[d], dst_ref=gathered.at[slot, d],
            send_sem=slow_send.at[d, j], recv_sem=slow_recv.at[d, slot],
            device_id={"freq": target}, device_id_type=MESH)

    halo_copy(0).start()
    for d in range(steps):
        for j in range(1, n):
            slow_copy(d, fi, j, lax.rem(fi + j, n)).start()

    lane = lax.broadcasted_iota(jnp.int32, (SUB, LANE), 1)
    lane_lo, lane_hi = lane == 0, lane == LANE - 1

    def recursion(d, order):
        here = d if order == 1 else steps - 2 + order
        before = d if order == 2 else steps - 3 + order
        to = steps - 1 + order
        last = order == TERMS - 1
        start = PAD + (PAD * ti if last else 0)
        count = rows // SUB + (0 if last else 1)

        def body(b, carry):
            at = pl.multiple_of(start + b * SUB, SUB)
            for f in range(4):
                twice, v = [], []
                for c in range(blocks):
                    mid = field[here, f, c, pl.ds(at, SUB), :]
                    two = mid + mid
                    twice.append(mid if order == 1 else two)
                    v.append((field[here, f, c, pl.ds(at - 1, SUB), :] + field[here, f, c, pl.ds(at + 1, SUB), :]) + two)
                q = []
                for c in range(blocks):
                    below = jnp.where(lane_hi, v[c - 1] if c > 0 else 0.0, v[c])
                    q.append(v[c] + pltpu.roll(below, 1, 1))
                for c in range(blocks):
                    if c + 1 < blocks:
                        above = pltpu.roll(jnp.where(lane_lo, q[c + 1], q[c]), LANE - 1, 1)
                    else:
                        above = jnp.where(lane_hi, v[c], pltpu.roll(q[c], LANE - 1, 1))
                    both = q[c] + above
                    if order == 1:
                        value = 0.125 * both - twice[c]
                    else:
                        value = 0.25 * both - (twice[c] + field[before, f, c, pl.ds(at, SUB), :])
                    field[to, f, c, pl.ds(at, SUB), :] = value
            return carry

        lax.fori_loop(0, count, body, 0)

    omega = omega_ref[0]
    per = LANE // cols

    def slow_tile(d, r, c):
        tiles = [gathered[c * per + q, d, pl.ds(r, SUB), :] for q in range(per)]
        return tiles[0] if per == 1 else jnp.concatenate(tiles, axis=1)

    def block_row(k):
        return pl.multiple_of(jnp.where(ti == 0, rows - (k + 1) * SUB, k * SUB), SUB)

    def accumulate(d, k):
        r = block_row(k)
        at = own(r)
        for c in range(blocks):
            h = folded_coefficients(slow_tile(d, r, c) * omega)
            sr = si = rr = ri = None
            for t in range(TERMS):
                slot = d if t == 0 else steps - 1 + t
                v = [field[slot, f, c, pl.ds(at, SUB), :] for f in range(4)]
                hv = [h[t] * x for x in v]
                if t == 0:
                    sr, si, rr, ri = hv
                elif t % 2 == 0:
                    sr, si, rr, ri = sr + hv[0], si + hv[1], rr + hv[2], ri + hv[3]
                else:
                    sr, si, rr, ri = sr - hv[1], si + hv[0], rr + hv[3], ri - hv[2]
            if d + 1 < steps:
                for f, x in enumerate((sr, si, rr, ri)):
                    field[d + 1, f, c, pl.ds(at, SUB), :] = x
            lanes = pl.ds(c * LANE, LANE)
            part[0, d, pl.ds(r, SUB), lanes] = sr * rr + si * ri
            part[1, d, pl.ds(r, SUB), lanes] = sr * sr + si * si

    per_unit = unit_rows // SUB
    unit_of_depth = rows // unit_rows

    def unit_at(u):
        d, k = u // unit_of_depth, u % unit_of_depth
        return d, pl.multiple_of(jnp.where(ti == 0, rows - (k + 1) * unit_rows, k * unit_rows), SUB)

    def unit_slice(u):
        d, r = unit_at(u)
        return d, pl.ds(r, unit_rows)

    def chunk_slice(u, z):
        d, r = unit_at(u)
        line = pl.multiple_of(r + SUB * lax.div(z, per_row), SUB)
        return d, pl.ds(line, SUB), pl.ds(pl.multiple_of(chunk_cols * lax.rem(z, per_row), LANE), chunk_cols)

    def s1_copy(u):
        at = unit_slice(u)
        return pltpu.make_async_remote_copy(
            src_ref=part.at[(other_y, *at)], dst_ref=recv1.at[at],
            send_sem=s1_send.at[u], recv_sem=s1_recv.at[u],
            device_id=freq_at(other_y, zi), device_id_type=MESH)

    def s2_copy(u, z, slot):
        return pltpu.make_async_remote_copy(
            src_ref=acc1.at[chunk_slice(u, z)], dst_ref=recv2.at[u, slot],
            send_sem=s2_send.at[u, z], recv_sem=s2_recv.at[u, slot],
            device_id=freq_at(yi, z), device_id_type=MESH)

    def piece(u, y, z):
        return result.at[(y, *chunk_slice(u, z))]

    def gz_copy(u, owner, target):
        return pltpu.make_async_remote_copy(
            src_ref=piece(u, yi, owner), dst_ref=piece(u, yi, owner),
            send_sem=gz_send.at[u, target], recv_sem=gz_recv.at[u, owner],
            device_id=freq_at(yi, target), device_id_type=MESH)

    def gy_copy(u, y, z):
        return pltpu.make_async_remote_copy(
            src_ref=piece(u, y, z), dst_ref=piece(u, y, z),
            send_sem=gy_send.at[u, z], recv_sem=gy_recv.at[u, z],
            device_id=freq_at(other_y, zi), device_id_type=MESH)

    peers = [lax.rem(zi + j, g2) for j in range(1, g2)]

    def stage_b(u):
        s1_copy(u).wait_recv()
        at = unit_slice(u)
        acc1[at] = part[(yi, *at)] + recv1[at]
        for z in peers:
            s2_copy(u, z, zi).start()

    scale = jnp.where(yi == 0, 1.0 / math.sqrt(freq_total), 1.0 / freq_total)

    def stage_c(u):
        for z in peers:
            s2_copy(u, zi, z).wait_recv()
        at = chunk_slice(u, zi)
        total = acc1[at]
        for z in peers:
            total = total + recv2[u, z]
        result[(yi, *at)] = total * scale
        for z in peers:
            gz_copy(u, zi, z).start()
        gy_copy(u, yi, zi).start()

    def stage_d(u):
        for z in peers:
            gz_copy(u, z, zi).wait_recv()
            gy_copy(u, yi, z).start()

    def out_copies(u):
        at = unit_slice(u)
        return [
            pltpu.make_async_copy(result.at[(0, *at)], image_ref.at[at], out_sem.at[0, u]),
            pltpu.make_async_copy(result.at[(1, *at)], energy_ref.at[at], out_sem.at[1, u]),
        ]

    def stage_e(u):
        for z in range(g2):
            gy_copy(u, other_y, z).wait_recv()
        for copy in out_copies(u):
            copy.start()

    stages = (stage_b, stage_c, stage_d, stage_e)
    queue = []
    clock = [0.0]

    def poll(us):
        clock[0] += us
        while queue and (us == math.inf or queue[0][0] <= clock[0]):
            _, u, stage = queue.pop(0)
            stages[stage](u)

    for d in range(steps):
        halo_copy(d).wait_recv()
        for order in range(1, TERMS):
            recursion(d, order)
            poll(ORDER_US)
        if d == 0:
            own_load.wait()
        for j in range(1, n):
            slow_copy(d, lax.rem(fi + j, n), j, fi).wait_recv()
        for k in range(rows // SUB):
            accumulate(d, k)
            if (k + 1) * SUB == HALO and d + 1 < steps:
                halo_copy(d + 1).start()
            if (k + 1) % per_unit == 0:
                u = d * unit_of_depth + k // per_unit
                s1_copy(u).start()
                queue.extend((clock[0] + lag, u, i) for i, lag in enumerate(LAGS))
                queue.sort()
            poll(ACC_US)
    poll(math.inf)

    for d in range(steps):
        halo_copy(d).wait_send()
        for j in range(1, n):
            slow_copy(d, fi, j, lax.rem(fi + j, n)).wait_send()
    for u in range(units):
        s1_copy(u).wait_send()
        for z in peers:
            s2_copy(u, z, zi).wait_send()
            gz_copy(u, zi, z).wait_send()
        for z in range(g2):
            gy_copy(u, yi, z).wait_send()
        for copy in out_copies(u):
            copy.wait()


def per_device(n, source_field, receiver_field, slowness, omegas):
    rows, width = source_field.shape[2:]
    steps, _, cols = slowness.shape
    g1 = 2
    g2 = n // g1
    blocks = width // LANE
    chunk_cols = max(LANE, width // g2)
    unit_rows = SUB * max(1, g2 * chunk_cols // width)
    units = steps * (rows // unit_rows)
    height = PAD + rows + HALO
    f32, dma = jnp.float32, pltpu.SemaphoreType.DMA
    src = source_field.reshape(2, rows, width)
    rec = receiver_field.reshape(2, rows, width)
    cfg = (n, g1, g2, rows, width, steps, omegas.shape[0] * n, cols, chunk_cols, unit_rows)
    any_spec = pl.BlockSpec(memory_space=pl.ANY)
    out = jax.ShapeDtypeStruct((steps, rows, width), f32)
    return pl.pallas_call(
        functools.partial(kernel, cfg),
        out_shape=(out, out),
        in_specs=[any_spec, any_spec, any_spec, pl.BlockSpec(memory_space=pltpu.SMEM)],
        out_specs=(any_spec, any_spec),
        scratch_shapes=[
            pltpu.VMEM((steps + TERMS - 1, 4, blocks, height, LANE), f32),
            pltpu.VMEM((n, steps, rows, cols), f32),
            pltpu.VMEM((2, steps, rows, width), f32),
            pltpu.VMEM((steps, rows, width), f32),
            pltpu.VMEM((steps, rows, width), f32),
            pltpu.VMEM((units, g2, SUB, chunk_cols), f32),
            pltpu.VMEM((2, steps, rows, width), f32),
            dma((2, blocks)), dma(()), dma((2, units)),
            dma((steps, n)), dma((steps, n)),
            dma((steps,)), dma((steps,)),
            dma((units,)), dma((units,)),
            dma((units, g2)), dma((units, g2)),
            dma((units, g2)), dma((units, g2)),
            dma((units, g2)), dma((units, g2)),
        ],
        compiler_params=pltpu.CompilerParams(
            collective_id=0, has_side_effects=True, vmem_limit_bytes=56 * 1024 * 1024),
    )(src, rec, slowness, omegas)


def solution(mesh):
    n = mesh.shape["freq"]
    assert mesh.shape["tile"] == 2 and n % 2 == 0
    in_specs = (
        P("shot", "freq", "tile", None),
        P("shot", "freq", "tile", None),
        P(None, "tile", "freq"),
        P("freq"),
    )
    out_specs = (P("shot", "tile", None), P("shot", "tile", None))
    return jax.shard_map(
        functools.partial(per_device, n), mesh=mesh, in_specs=in_specs, out_specs=out_specs,
        check_vma=False,
    )
```

```python
import functools
import math

import jax
import jax.numpy as jnp
import numpy as np
from jax import lax
from jax.experimental import pallas as pl
from jax.experimental.pallas import tpu as pltpu
from jax.sharding import PartitionSpec as P

TERMS = 10
NODES = 16
HALF = NODES // 2
SUB, LANE = 8, 128
HALO = 16
PAD = 8
MESH = pl.DeviceIdType.MESH
ORDER_US, ACC_US = 0.43, 0.45
SPLITS = (1, 4, 7, TERMS)
LAGS = (3.0, 7.0, 11.0, 14.0)
QUEUE_US = 0.8

SIN_POLY = (3.14159258, -5.16770688, 2.55003137, -0.59804516, 0.07722009)
COS_POLY = (0.99999995, -4.93479286, 4.0584119, -1.33188005, 0.21969657)


def horner(coefs, z):
    out = coefs[-1] * z + coefs[-2]
    for c in reversed(coefs[:-2]):
        out = out * z + c
    return out


def folded_coefficients(u):
    theta = [math.pi * (m + 0.5) / NODES for m in range(HALF)]
    cosines, sines = [], []
    for m in range(HALF):
        y = u * (math.cos(theta[m]) / (2 * math.pi))
        g = y - jnp.round(y)
        z = g * g
        s = horner(SIN_POLY, z) * g
        c = horner(COS_POLY, z)
        twice = s + s
        cosines.append(1.0 - twice * s)
        sines.append(twice * c)
    weight = [2.0 * (1.0 if n == 0 else 2.0) / NODES for n in range(TERMS)]
    out = [None] * TERMS
    sums = [cosines[m] + cosines[HALF - 1 - m] for m in range(HALF // 2)]
    diffs = [cosines[m] - cosines[HALF - 1 - m] for m in range(HALF // 2)]
    for n in range(0, TERMS, 2):
        terms = sums if (n // 2) % 2 == 0 else diffs
        total = None
        for m in range(HALF // 2):
            term = terms[m] * (weight[n] * math.cos(n * theta[m]))
            total = term if total is None else total + term
        out[n] = total
    for n in range(1, TERMS, 2):
        total = None
        for m in range(HALF):
            term = sines[m] * (weight[n] * math.cos(n * theta[m]))
            total = term if total is None else total + term
        out[n] = total
    return out


def kernel(cfg, src_ref, rec_ref, slow_ref, omega_ref, result, field, gathered, part,
           recv1, acc1, recv2, load_sem, own_sem, slow_send, slow_recv, forward_send,
           halo_send, halo_recv, s1_send, s1_recv, s2_send, s2_recv,
           gz_send, gz_recv, gy_send, gy_recv):
    n, g1, g2, rows, width, steps, freq_total, cols = cfg
    blocks = width // LANE
    half = width // 2
    depth_units = rows // SUB
    units = steps * depth_units
    owners = (g2 // 2 - 1, g2 // 2)
    fi = lax.axis_index("freq")
    ti = lax.axis_index("tile")
    yi, zi = lax.rem(fi, g1), lax.div(fi, g1)
    other_y = g1 - 1 - yi

    def freq_at(y, z):
        return {"freq": z * g1 + y}

    def own(r):
        return pl.multiple_of(PAD + PAD * ti + r, SUB)

    def base(d):
        return d % 2 * TERMS

    loads = []
    for c in range(blocks):
        lanes = pl.ds(c * LANE, LANE)
        loads.append(pltpu.make_async_copy(
            src_ref.at[:, :, lanes], field.at[0, 0:2, c, pl.ds(own(0), rows)], load_sem.at[0, c]))
        loads.append(pltpu.make_async_copy(
            rec_ref.at[:, :, lanes], field.at[0, 2:4, c, pl.ds(own(0), rows)], load_sem.at[1, c]))
    own_load = pltpu.make_async_copy(slow_ref, gathered.at[fi], own_sem)
    for copy in loads:
        copy.start()
    own_load.start()

    barrier = pltpu.get_barrier_semaphore()
    peers = [lax.rem(zi + j, g2) for j in range(1, g2)]
    for z in peers:
        pl.semaphore_signal(barrier, inc=1, device_id=freq_at(yi, z), device_id_type=MESH)
    pl.semaphore_signal(barrier, inc=1, device_id=freq_at(other_y, zi), device_id_type=MESH)
    pl.semaphore_signal(barrier, inc=1, device_id={"tile": 1 - ti}, device_id_type=MESH)

    zero = jnp.zeros((4, blocks, SUB, LANE), jnp.float32)
    low, high = pl.ds(0, SUB), pl.ds(PAD + rows + SUB, SUB)
    edge = pl.ds(pl.multiple_of((PAD + rows + SUB) * ti, SUB), SUB)
    for d in range(min(steps, 2)):
        field[base(d), :, :, edge, :] = zero
        for t in range(1, TERMS):
            field[base(d) + t, :, :, low, :] = zero
            field[base(d) + t, :, :, high, :] = zero

    for copy in loads:
        copy.wait()
    pl.semaphore_wait(barrier, g2 + 1)

    def halo_copy(d):
        src = pl.multiple_of(jnp.where(ti == 0, PAD + rows - HALO, PAD + PAD), SUB)
        far = pl.multiple_of(jnp.where(ti == 0, 0, PAD + rows), SUB)
        return pltpu.make_async_remote_copy(
            src_ref=field.at[base(d), :, :, pl.ds(src, HALO)], dst_ref=field.at[base(d), :, :, pl.ds(far, HALO)],
            send_sem=halo_send.at[d], recv_sem=halo_recv.at[d],
            device_id={"tile": 1 - ti}, device_id_type=MESH)

    def slow_copy(d, owner, target):
        return pltpu.make_async_remote_copy(
            src_ref=slow_ref.at[d], dst_ref=gathered.at[owner * g1 + yi, d],
            send_sem=slow_send.at[d, target], recv_sem=slow_recv.at[d, owner * g1 + yi],
            device_id=freq_at(yi, target), device_id_type=MESH)

    def forward_copy(d, y, z):
        slot = z * g1 + y
        return pltpu.make_async_remote_copy(
            src_ref=gathered.at[slot, d], dst_ref=gathered.at[slot, d],
            send_sem=forward_send.at[d, z], recv_sem=slow_recv.at[d, slot],
            device_id=freq_at(other_y, zi), device_id_type=MESH)

    def send_slowness(d):
        for z in peers:
            slow_copy(d, zi, z).start()
        forward_copy(d, yi, zi).start()

    def forward_slowness(d):
        for z in peers:
            slow_copy(d, z, zi).wait_recv()
            forward_copy(d, yi, z).start()

    own_load.wait()
    send_slowness(0)
    halo_copy(0).start()

    lane = lax.broadcasted_iota(jnp.int32, (SUB, LANE), 1)
    lane_lo, lane_hi = lane == 0, lane == LANE - 1

    def recursion(at, first):
        for b in range(rows // SUB + 1):
            for f in range(4):
                if first:
                    tile_row(at, None, at + 1, f, PAD + b * SUB)
                else:
                    tile_row(at + 1, at, at + 2, f, PAD + b * SUB)

    def tile_row(here, before, to, f, at):
        v = []
        for c in range(blocks):
            mid = field[here, f, c, at:at + SUB, :]
            v.append((field[here, f, c, at - 1:at - 1 + SUB, :] + field[here, f, c, at + 1:at + 1 + SUB, :]) + (mid + mid))
        left = [pltpu.roll(x, 1, 1) for x in v]
        right = [pltpu.roll(x, LANE - 1, 1) for x in v]
        for c in range(blocks):
            low_side = jnp.where(lane_lo, left[c - 1] if c > 0 else 0.0, left[c])
            high_side = jnp.where(lane_hi, right[c + 1] if c + 1 < blocks else 0.0, right[c])
            both = (low_side + high_side) + (v[c] + v[c])
            mid = field[here, f, c, at:at + SUB, :]
            if before is None:
                value = 0.125 * both - mid
            else:
                value = 0.25 * both - ((mid + mid) + field[before, f, c, at:at + SUB, :])
            field[to, f, c, at:at + SUB, :] = value

    def recursions(d, lo, hi):
        def body(at, carry):
            recursion(at, False)
            return carry

        if lo == 1:
            recursion(base(d), True)
            lo = 2
        if hi > lo:
            lax.fori_loop(base(d) + lo - 2, base(d) + hi - 2, body, 0)

    omega = omega_ref[0]
    per = LANE // cols

    def slow_tile(d, r, c):
        tiles = [gathered[c * per + q, d, pl.ds(r, SUB), :] for q in range(per)]
        return tiles[0] if per == 1 else jnp.concatenate(tiles, axis=1)

    def block_row(k):
        return pl.multiple_of(jnp.where(ti == 0, rows - (k + 1) * SUB, k * SUB), SUB)

    def accumulate(d, k):
        r = block_row(k)
        at = own(r)
        for c in range(blocks):
            h = folded_coefficients(slow_tile(d, r, c) * omega)
            sr = si = rr = ri = None
            for t in range(TERMS):
                v = [field[base(d) + t, f, c, pl.ds(at, SUB), :] for f in range(4)]
                hv = [h[t] * x for x in v]
                if t == 0:
                    sr, si, rr, ri = hv
                elif t % 2 == 0:
                    sr, si, rr, ri = sr + hv[0], si + hv[1], rr + hv[2], ri + hv[3]
                else:
                    sr, si, rr, ri = sr - hv[1], si + hv[0], rr + hv[3], ri - hv[2]
            if d + 1 < steps:
                for f, x in enumerate((sr, si, rr, ri)):
                    field[base(d + 1), f, c, pl.ds(at, SUB), :] = x
            lanes = pl.ds(c * LANE, LANE)
            part[0, d, pl.ds(r, SUB), lanes] = sr * rr + si * ri
            part[1, d, pl.ds(r, SUB), lanes] = sr * sr + si * si

    def unit_slice(u):
        return u // depth_units, pl.ds(block_row(u % depth_units), SUB)

    def half_slice(u, h):
        return (*unit_slice(u), slice(h * half, (h + 1) * half))

    def s1_copy(u):
        at = unit_slice(u)
        return pltpu.make_async_remote_copy(
            src_ref=part.at[(other_y, *at)], dst_ref=recv1.at[at],
            send_sem=s1_send.at[u], recv_sem=s1_recv.at[u],
            device_id=freq_at(other_y, zi), device_id_type=MESH)

    def s2_copy(u, h, slot):
        return pltpu.make_async_remote_copy(
            src_ref=acc1.at[half_slice(u, h)], dst_ref=recv2.at[u, slot],
            send_sem=s2_send.at[u, h], recv_sem=s2_recv.at[u, slot],
            device_id=freq_at(yi, owners[h]), device_id_type=MESH)

    def piece(u, y, h):
        return result.at[(y, *half_slice(u, h))]

    def gz_copy(u, h, target):
        return pltpu.make_async_remote_copy(
            src_ref=piece(u, yi, h), dst_ref=piece(u, yi, h),
            send_sem=gz_send.at[u, target], recv_sem=gz_recv.at[u, h],
            device_id=freq_at(yi, target), device_id_type=MESH)

    def gy_copy(u, y, h):
        return pltpu.make_async_remote_copy(
            src_ref=piece(u, y, h), dst_ref=piece(u, y, h),
            send_sem=gy_send.at[u, h], recv_sem=gy_recv.at[u, h],
            device_id=freq_at(other_y, zi), device_id_type=MESH)

    def stage_b(u):
        s1_copy(u).wait_recv()
        at = unit_slice(u)
        acc1[at] = part[(yi, *at)] + recv1[at]
        for h, owner in enumerate(owners):
            @pl.when(zi != owner)
            def _():
                s2_copy(u, h, zi).start()

    scale = jnp.where(yi == 0, 1.0 / math.sqrt(freq_total), 1.0 / freq_total)

    def stage_c(u):
        for h, owner in enumerate(owners):
            @pl.when(zi == owner)
            def _():
                others = [z for z in range(g2) if z != owner]
                for z in others:
                    s2_copy(u, h, z).wait_recv()
                at = half_slice(u, h)
                total = acc1[at]
                for z in others:
                    total = total + recv2[u, z]
                result[(yi, *at)] = total * scale
                for z in sorted(others, key=lambda z: -abs(z - owner)):
                    gz_copy(u, h, z).start()
                gy_copy(u, yi, h).start()

    def stage_d(u):
        for h, owner in enumerate(owners):
            @pl.when(zi != owner)
            def _():
                gz_copy(u, h, zi).wait_recv()
                gy_copy(u, yi, h).start()

    def stage_e(u):
        for h in range(2):
            gy_copy(u, other_y, h).wait_recv()

    stages = (stage_b, stage_c, stage_d, stage_e)
    queue = []
    clock = [0.0]

    def poll(us):
        clock[0] += us
        while queue and (us == math.inf or queue[0][0] <= clock[0]):
            _, u, stage = queue.pop(0)
            stages[stage](u)

    for d in range(steps):
        halo_copy(d).wait_recv()
        for lo, hi in zip(SPLITS[:-1], SPLITS[1:]):
            recursions(d, lo, hi)
            if d == 0 and lo == SPLITS[-3]:
                forward_slowness(0)
                for later in range(1, steps):
                    send_slowness(later)
            poll(ORDER_US * (hi - lo))
        halo_copy(d).wait_send()
        for z in range(g2):
            forward_copy(d, other_y, z).wait_recv()
        for k in range(depth_units):
            accumulate(d, k)
            if (k + 1) * SUB == HALO and d + 1 < steps:
                halo_copy(d + 1).start()
            u = d * depth_units + k
            s1_copy(u).start()
            queue.extend((clock[0] + lag + QUEUE_US * k, u, i) for i, lag in enumerate(LAGS))
            queue.sort()
            poll(ACC_US)
        if d == 0:
            for later in range(1, steps):
                forward_slowness(later)
    poll(math.inf)

    for d in range(steps):
        for z in peers:
            slow_copy(d, zi, z).wait_send()
        for z in range(g2):
            forward_copy(d, yi, z).wait_send()
    for u in range(units):
        s1_copy(u).wait_send()
        for h, owner in enumerate(owners):
            @pl.when(zi != owner)
            def _():
                s2_copy(u, h, zi).wait_send()

            @pl.when(zi == owner)
            def _():
                for z in range(g2):
                    if z != owner:
                        gz_copy(u, h, z).wait_send()

            gy_copy(u, yi, h).wait_send()


def per_device(n, source_field, receiver_field, slowness, omegas):
    rows, width = source_field.shape[2:]
    steps, _, cols = slowness.shape
    g1 = 2
    g2 = n // g1
    blocks = width // LANE
    units = steps * (rows // SUB)
    height = PAD + rows + HALO
    f32, dma = jnp.float32, pltpu.SemaphoreType.DMA
    src = source_field.reshape(2, rows, width)
    rec = receiver_field.reshape(2, rows, width)
    cfg = (n, g1, g2, rows, width, steps, omegas.shape[0] * n, cols)
    any_spec = pl.BlockSpec(memory_space=pl.ANY)
    out = pl.pallas_call(
        functools.partial(kernel, cfg),
        out_shape=jax.ShapeDtypeStruct((2, steps, rows, width), f32),
        in_specs=[any_spec, any_spec, any_spec, pl.BlockSpec(memory_space=pltpu.SMEM)],
        out_specs=pl.BlockSpec(memory_space=pltpu.VMEM),
        scratch_shapes=[
            pltpu.VMEM((2 * TERMS, 4, blocks, height, LANE), f32),
            pltpu.VMEM((n, steps, rows, cols), f32),
            pltpu.VMEM((2, steps, rows, width), f32),
            pltpu.VMEM((steps, rows, width), f32),
            pltpu.VMEM((steps, rows, width), f32),
            pltpu.VMEM((units, g2, SUB, width // 2), f32),
            dma((2, blocks)), dma(()),
            dma((steps, g2)), dma((steps, n)), dma((steps, g2)),
            dma((steps,)), dma((steps,)),
            dma((units,)), dma((units,)),
            dma((units, 2)), dma((units, g2)),
            dma((units, g2)), dma((units, 2)),
            dma((units, 2)), dma((units, 2)),
        ],
        compiler_params=pltpu.CompilerParams(
            collective_id=0, has_side_effects=True, vmem_limit_bytes=56 * 1024 * 1024),
    )(src, rec, slowness, omegas)
    return out[0], out[1]


def solution(mesh):
    n = mesh.shape["freq"]
    assert mesh.shape["tile"] == 2 and n % 4 == 0
    in_specs = (
        P("shot", "freq", "tile", None),
        P("shot", "freq", "tile", None),
        P(None, "tile", "freq"),
        P("freq"),
    )
    out_specs = (P("shot", "tile", None), P("shot", "tile", None))
    return jax.shard_map(
        functools.partial(per_device, n), mesh=mesh, in_specs=in_specs, out_specs=out_specs,
        check_vma=False,
    )
```

```python
import functools
import math

import jax
import jax.numpy as jnp
import numpy as np
from jax import lax
from jax.experimental import pallas as pl
from jax.experimental.pallas import tpu as pltpu
from jax.sharding import PartitionSpec as P

TERMS = 10
NODES = 16
HALF = NODES // 2
SUB, LANE = 8, 128
HALO = 16
PAD = 8
MESH = pl.DeviceIdType.MESH
ORDER_US, ACC_US = 0.43, 0.45
SPLITS = (1, 4, 7, TERMS)
LAGS = (3.0, 7.0, 11.0, 99.0)
QUEUE_US = 0.8

SIN_POLY = (3.14159258, -5.16770688, 2.55003137, -0.59804516, 0.07722009)
COS_POLY = (0.99999995, -4.93479286, 4.0584119, -1.33188005, 0.21969657)


def horner(coefs, z):
    out = coefs[-1] * z + coefs[-2]
    for c in reversed(coefs[:-2]):
        out = out * z + c
    return out


def folded_coefficients(u):
    theta = [math.pi * (m + 0.5) / NODES for m in range(HALF)]
    cosines, sines = [], []
    for m in range(HALF):
        y = u * (math.cos(theta[m]) / (2 * math.pi))
        g = y - jnp.round(y)
        z = g * g
        s = horner(SIN_POLY, z) * g
        c = horner(COS_POLY, z)
        twice = s + s
        cosines.append(1.0 - twice * s)
        sines.append(twice * c)
    weight = [2.0 * (1.0 if n == 0 else 2.0) / NODES for n in range(TERMS)]
    out = [None] * TERMS
    sums = [cosines[m] + cosines[HALF - 1 - m] for m in range(HALF // 2)]
    diffs = [cosines[m] - cosines[HALF - 1 - m] for m in range(HALF // 2)]
    for n in range(0, TERMS, 2):
        terms = sums if (n // 2) % 2 == 0 else diffs
        total = None
        for m in range(HALF // 2):
            term = terms[m] * (weight[n] * math.cos(n * theta[m]))
            total = term if total is None else total + term
        out[n] = total
    for n in range(1, TERMS, 2):
        total = None
        for m in range(HALF):
            term = sines[m] * (weight[n] * math.cos(n * theta[m]))
            total = term if total is None else total + term
        out[n] = total
    return out


def kernel(cfg, src_ref, rec_ref, slow_ref, omega_ref, result, field, gathered, part,
           recv1, acc1, recv2, load_sem, own_sem, slow_send, slow_recv, forward_send,
           halo_send, halo_recv, s1_send, s1_recv, s2_send, s2_recv,
           gz_send, gz_recv, gy_send, gy_recv):
    n, g1, g2, rows, width, steps, freq_total, cols = cfg
    blocks = width // LANE
    half = width // 2
    depth_units = rows // SUB
    units = steps * depth_units
    owners = (g2 // 2 - 1, g2 // 2)
    fi = lax.axis_index("freq")
    ti = lax.axis_index("tile")
    yi, zi = lax.rem(fi, g1), lax.div(fi, g1)
    other_y = g1 - 1 - yi

    def freq_at(y, z):
        return {"freq": z * g1 + y}

    def own(r):
        return pl.multiple_of(PAD + PAD * ti + r, SUB)

    def base(d):
        return d % 2 * TERMS

    loads = []
    for c in range(blocks):
        lanes = pl.ds(c * LANE, LANE)
        loads.append(pltpu.make_async_copy(
            src_ref.at[:, :, lanes], field.at[0, 0:2, c, pl.ds(own(0), rows)], load_sem.at[0, c]))
        loads.append(pltpu.make_async_copy(
            rec_ref.at[:, :, lanes], field.at[0, 2:4, c, pl.ds(own(0), rows)], load_sem.at[1, c]))
    own_load = pltpu.make_async_copy(slow_ref, gathered.at[fi], own_sem)
    for copy in loads:
        copy.start()
    own_load.start()

    barrier = pltpu.get_barrier_semaphore()
    peers = [lax.rem(zi + j, g2) for j in range(1, g2)]
    for z in peers:
        pl.semaphore_signal(barrier, inc=1, device_id=freq_at(yi, z), device_id_type=MESH)
    pl.semaphore_signal(barrier, inc=1, device_id=freq_at(other_y, zi), device_id_type=MESH)
    pl.semaphore_signal(barrier, inc=1, device_id={"tile": 1 - ti}, device_id_type=MESH)

    zero = jnp.zeros((4, blocks, SUB, LANE), jnp.float32)
    low, high = pl.ds(0, SUB), pl.ds(PAD + rows + SUB, SUB)
    edge = pl.ds(pl.multiple_of((PAD + rows + SUB) * ti, SUB), SUB)
    for d in range(min(steps, 2)):
        field[base(d), :, :, edge, :] = zero
        for t in range(1, TERMS):
            field[base(d) + t, :, :, low, :] = zero
            field[base(d) + t, :, :, high, :] = zero

    for copy in loads:
        copy.wait()
    pl.semaphore_wait(barrier, g2 + 1)

    def halo_copy(d):
        src = pl.multiple_of(jnp.where(ti == 0, PAD + rows - HALO, PAD + PAD), SUB)
        far = pl.multiple_of(jnp.where(ti == 0, 0, PAD + rows), SUB)
        return pltpu.make_async_remote_copy(
            src_ref=field.at[base(d), :, :, pl.ds(src, HALO)], dst_ref=field.at[base(d), :, :, pl.ds(far, HALO)],
            send_sem=halo_send.at[d], recv_sem=halo_recv.at[d],
            device_id={"tile": 1 - ti}, device_id_type=MESH)

    def slow_copy(d, owner, target):
        return pltpu.make_async_remote_copy(
            src_ref=slow_ref.at[d], dst_ref=gathered.at[owner * g1 + yi, d],
            send_sem=slow_send.at[d, target], recv_sem=slow_recv.at[d, owner * g1 + yi],
            device_id=freq_at(yi, target), device_id_type=MESH)

    def forward_copy(d, y, z):
        slot = z * g1 + y
        return pltpu.make_async_remote_copy(
            src_ref=gathered.at[slot, d], dst_ref=gathered.at[slot, d],
            send_sem=forward_send.at[d, z], recv_sem=slow_recv.at[d, slot],
            device_id=freq_at(other_y, zi), device_id_type=MESH)

    def send_slowness(d):
        for z in peers:
            slow_copy(d, zi, z).start()
        forward_copy(d, yi, zi).start()

    def forward_slowness(d):
        for z in peers:
            slow_copy(d, z, zi).wait_recv()
            forward_copy(d, yi, z).start()

    own_load.wait()
    send_slowness(0)
    halo_copy(0).start()

    lane = lax.broadcasted_iota(jnp.int32, (SUB, LANE), 1)
    lane_lo, lane_hi = lane == 0, lane == LANE - 1

    def recursion(at, first):
        for b in range(rows // SUB + 1):
            for f in range(4):
                if first:
                    tile_row(at, None, at + 1, f, PAD + b * SUB)
                else:
                    tile_row(at + 1, at, at + 2, f, PAD + b * SUB)

    def tile_row(here, before, to, f, at):
        v = []
        for c in range(blocks):
            mid = field[here, f, c, at:at + SUB, :]
            v.append((field[here, f, c, at - 1:at - 1 + SUB, :] + field[here, f, c, at + 1:at + 1 + SUB, :]) + (mid + mid))
        left = [pltpu.roll(x, 1, 1) for x in v]
        right = [pltpu.roll(x, LANE - 1, 1) for x in v]
        for c in range(blocks):
            low_side = jnp.where(lane_lo, left[c - 1] if c > 0 else 0.0, left[c])
            high_side = jnp.where(lane_hi, right[c + 1] if c + 1 < blocks else 0.0, right[c])
            both = (low_side + high_side) + (v[c] + v[c])
            mid = field[here, f, c, at:at + SUB, :]
            if before is None:
                value = 0.125 * both - mid
            else:
                value = 0.25 * both - ((mid + mid) + field[before, f, c, at:at + SUB, :])
            field[to, f, c, at:at + SUB, :] = value

    def recursions(d, lo, hi):
        def body(at, carry):
            recursion(at, False)
            return carry

        if lo == 1:
            recursion(base(d), True)
            lo = 2
        if hi > lo:
            lax.fori_loop(base(d) + lo - 2, base(d) + hi - 2, body, 0)

    omega = omega_ref[0]
    per = LANE // cols

    def slow_tile(d, r, c):
        tiles = [gathered[c * per + q, d, pl.ds(r, SUB), :] for q in range(per)]
        return tiles[0] if per == 1 else jnp.concatenate(tiles, axis=1)

    def block_row(k):
        return pl.multiple_of(jnp.where(ti == 0, rows - (k + 1) * SUB, k * SUB), SUB)

    def accumulate(d, k):
        r = block_row(k)
        at = own(r)
        for c in range(blocks):
            h = folded_coefficients(slow_tile(d, r, c) * omega)
            sr = si = rr = ri = None
            for t in range(TERMS):
                v = [field[base(d) + t, f, c, pl.ds(at, SUB), :] for f in range(4)]
                hv = [h[t] * x for x in v]
                if t == 0:
                    sr, si, rr, ri = hv
                elif t % 2 == 0:
                    sr, si, rr, ri = sr + hv[0], si + hv[1], rr + hv[2], ri + hv[3]
                else:
                    sr, si, rr, ri = sr - hv[1], si + hv[0], rr + hv[3], ri - hv[2]
            if d + 1 < steps:
                for f, x in enumerate((sr, si, rr, ri)):
                    field[base(d + 1), f, c, pl.ds(at, SUB), :] = x
            lanes = pl.ds(c * LANE, LANE)
            part[0, d, pl.ds(r, SUB), lanes] = sr * rr + si * ri
            part[1, d, pl.ds(r, SUB), lanes] = sr * sr + si * si

    def unit_slice(u):
        return u // depth_units, pl.ds(block_row(u % depth_units), SUB)

    def half_slice(u, h):
        return (*unit_slice(u), slice(h * half, (h + 1) * half))

    def s1_copy(u):
        at = unit_slice(u)
        return pltpu.make_async_remote_copy(
            src_ref=part.at[(other_y, *at)], dst_ref=recv1.at[at],
            send_sem=s1_send.at[u], recv_sem=s1_recv.at[u],
            device_id=freq_at(other_y, zi), device_id_type=MESH)

    def s2_copy(u, h, slot):
        return pltpu.make_async_remote_copy(
            src_ref=acc1.at[half_slice(u, h)], dst_ref=recv2.at[u, slot],
            send_sem=s2_send.at[u, h], recv_sem=s2_recv.at[u, slot],
            device_id=freq_at(yi, owners[h]), device_id_type=MESH)

    def piece(u, y, h):
        return result.at[(y, *half_slice(u, h))]

    def gz_copy(u, h, target):
        return pltpu.make_async_remote_copy(
            src_ref=piece(u, yi, h), dst_ref=piece(u, yi, h),
            send_sem=gz_send.at[u, target], recv_sem=gz_recv.at[u, h],
            device_id=freq_at(yi, target), device_id_type=MESH)

    def gy_copy(u, y, h):
        return pltpu.make_async_remote_copy(
            src_ref=piece(u, y, h), dst_ref=piece(u, y, h),
            send_sem=gy_send.at[u, h], recv_sem=gy_recv.at[u, h],
            device_id=freq_at(other_y, zi), device_id_type=MESH)

    def stage_b(u):
        s1_copy(u).wait_recv()
        at = unit_slice(u)
        acc1[at] = part[(yi, *at)] + recv1[at]
        for h, owner in enumerate(owners):
            @pl.when(zi != owner)
            def _():
                s2_copy(u, h, zi).start()

    scale = jnp.where(yi == 0, 1.0 / math.sqrt(freq_total), 1.0 / freq_total)

    def stage_c(u):
        for h, owner in enumerate(owners):
            @pl.when(zi == owner)
            def _():
                others = [z for z in range(g2) if z != owner]
                for z in others:
                    s2_copy(u, h, z).wait_recv()
                at = half_slice(u, h)
                total = acc1[at]
                for z in others:
                    total = total + recv2[u, z]
                result[(yi, *at)] = total * scale
                for z in sorted(others, key=lambda z: -abs(z - owner)):
                    gz_copy(u, h, z).start()
                gy_copy(u, yi, h).start()

    def stage_d(u):
        for h, owner in enumerate(owners):
            @pl.when(zi != owner)
            def _():
                gz_copy(u, h, zi).wait_recv()
                gy_copy(u, yi, h).start()

    def stage_e(u):
        for h in range(2):
            gy_copy(u, other_y, h).wait_recv()

    stages = (stage_b, stage_c, stage_d, stage_e)
    queue = []
    clock = [0.0]

    def poll(us):
        clock[0] += us
        while queue and (us == math.inf or queue[0][0] <= clock[0]):
            _, u, stage = queue.pop(0)
            stages[stage](u)

    for d in range(steps):
        halo_copy(d).wait_recv()
        for lo, hi in zip(SPLITS[:-1], SPLITS[1:]):
            recursions(d, lo, hi)
            if d == 0 and lo == SPLITS[-3]:
                forward_slowness(0)
                for later in range(1, steps):
                    send_slowness(later)
            poll(ORDER_US * (hi - lo))
        halo_copy(d).wait_send()
        for z in range(g2):
            forward_copy(d, other_y, z).wait_recv()
        for k in range(depth_units):
            accumulate(d, k)
            if (k + 1) * SUB == HALO and d + 1 < steps:
                halo_copy(d + 1).start()
            u = d * depth_units + k
            s1_copy(u).start()
            queue.extend((clock[0] + lag + QUEUE_US * k, u, i) for i, lag in enumerate(LAGS))
            queue.sort()
            poll(ACC_US)
        if d == 0:
            for later in range(1, steps):
                forward_slowness(later)
    poll(math.inf)

    for d in range(steps):
        for z in peers:
            slow_copy(d, zi, z).wait_send()
        for z in range(g2):
            forward_copy(d, yi, z).wait_send()
    for u in range(units):
        s1_copy(u).wait_send()
        for h, owner in enumerate(owners):
            @pl.when(zi != owner)
            def _():
                s2_copy(u, h, zi).wait_send()

            @pl.when(zi == owner)
            def _():
                for z in range(g2):
                    if z != owner:
                        gz_copy(u, h, z).wait_send()

            gy_copy(u, yi, h).wait_send()


def per_device(n, source_field, receiver_field, slowness, omegas):
    rows, width = source_field.shape[2:]
    steps, _, cols = slowness.shape
    g1 = 2
    g2 = n // g1
    blocks = width // LANE
    units = steps * (rows // SUB)
    height = PAD + rows + HALO
    f32, dma = jnp.float32, pltpu.SemaphoreType.DMA
    src = source_field.reshape(2, rows, width)
    rec = receiver_field.reshape(2, rows, width)
    cfg = (n, g1, g2, rows, width, steps, omegas.shape[0] * n, cols)
    any_spec = pl.BlockSpec(memory_space=pl.ANY)
    out = pl.pallas_call(
        functools.partial(kernel, cfg),
        out_shape=jax.ShapeDtypeStruct((2, steps, rows, width), f32),
        in_specs=[any_spec, any_spec, any_spec, pl.BlockSpec(memory_space=pltpu.SMEM)],
        out_specs=pl.BlockSpec(memory_space=pltpu.VMEM),
        scratch_shapes=[
            pltpu.VMEM((2 * TERMS, 4, blocks, height, LANE), f32),
            pltpu.VMEM((n, steps, rows, cols), f32),
            pltpu.VMEM((2, steps, rows, width), f32),
            pltpu.VMEM((steps, rows, width), f32),
            pltpu.VMEM((steps, rows, width), f32),
            pltpu.VMEM((units, g2, SUB, width // 2), f32),
            dma((2, blocks)), dma(()),
            dma((steps, g2)), dma((steps, n)), dma((steps, g2)),
            dma((steps,)), dma((steps,)),
            dma((units,)), dma((units,)),
            dma((units, 2)), dma((units, g2)),
            dma((units, g2)), dma((units, 2)),
            dma((units, 2)), dma((units, 2)),
        ],
        compiler_params=pltpu.CompilerParams(
            collective_id=0, has_side_effects=True, vmem_limit_bytes=56 * 1024 * 1024),
    )(src, rec, slowness, omegas)
    return out[0], out[1]


def solution(mesh):
    n = mesh.shape["freq"]
    assert mesh.shape["tile"] == 2 and n % 4 == 0
    in_specs = (
        P("shot", "freq", "tile", None),
        P("shot", "freq", "tile", None),
        P(None, "tile", "freq"),
        P("freq"),
    )
    out_specs = (P("shot", "tile", None), P("shot", "tile", None))
    return jax.shard_map(
        functools.partial(per_device, n), mesh=mesh, in_specs=in_specs, out_specs=out_specs,
        check_vma=False,
    )
```
